32 devices in a mesh: dp: 8 (over z, x), ctx: 4 (over y, core).
Axes of the slice: x: 2, y: 2, z: 4, core: 2. Of those that a mesh axis runs over, the one named last changes fastest.
Arguments:
- tokens: bfloat16 [16, 1024, 768], P('dp', 'ctx'), may hold values from -6 to 6
- segment_ids: int32 [16, 1024], P('dp', 'ctx'), may hold values from 0 to 3, never falling along the last dimension, each value on 1 to 512 neighbouring positions
- cotangent: bfloat16 [16, 1024, 768], P('dp', 'ctx'), may hold values from -6 to 6
- w_in: float32 [768, 3352], P(('dp', 'ctx')), may hold values from -0.21875 to 0.21875
- w_out: float32 [1536, 768], P(('dp', 'ctx')), may hold values from -0.15625 to 0.15625
- mom_in: float32 [768, 3352], P(('dp', 'ctx')), may hold values from -128 to 128
- mom_out: float32 [1536, 768], P(('dp', 'ctx')), may hold values from -640 to 640
- pre_gain: float32 [768], replicated, may hold values from 0.5 to 1.5
- conv_weight: float32 [4, 1792], replicated, may hold values from -3 to 3
- conv_bias: float32 [1792], replicated, may hold values from -6 to 6
- dt_bias: float32 [24], replicated, may hold values from -5 to -3
- a_log: float32 [24], replicated, may hold values from -3.5 to 1.1
- d_skip: float32 [24], replicated, may hold values from 0.5 to 1.5
- norm_gain: float32 [1536], replicated, may hold values from 0.5 to 1.5
Outputs:
- mixed: bfloat16 [16, 1024, 768], P('dp', 'ctx')
- d_tokens: bfloat16 [16, 1024, 768], P('dp', 'ctx')
- grad_w_in: float32 [768, 3352], P(('dp', 'ctx'))
- grad_w_out: float32 [1536, 768], P(('dp', 'ctx'))
- grad_pre_gain: float32 [768], replicated
- grad_conv_weight: float32 [4, 1792], replicated
- grad_conv_bias: float32 [1792], replicated
- grad_dt_bias: float32 [24], replicated
- grad_a_log: float32 [24], replicated
- grad_d_skip: float32 [24], replicated
- grad_norm_gain: float32 [1536], replicated
- new_w_in: float32 [768, 3352], P(('dp', 'ctx'))
- new_w_out: float32 [1536, 768], P(('dp', 'ctx'))
- new_mom_in: float32 [768, 3352], P(('dp', 'ctx'))
- new_mom_out: float32 [1536, 768], P(('dp', 'ctx'))
- new_pre_gain: float32 [768], replicated
- new_conv_weight: float32 [4, 1792], replicated
- new_conv_bias: float32 [1792], replicated
- new_dt_bias: float32 [24], replicated
- new_a_log: float32 [24], replicated
- new_d_skip: float32 [24], replicated
- new_norm_gain: float32 [1536], replicated
The draws below stay inside these ranges and needn't reach their ends.
Inputs may be any that keep to these rules, and one draw needn't show every extreme that they name: `segment_ids`: segment numbers never fall along a sequence; each document has 1 to 512 tokens and one has exactly 512.
All inputs are finite; a program needn't handle non-finite values.
Results may differ from the reference program's by a relative error of at most 0.01.
Values may be sent and summed in bfloat16 or wider, within the bound.
No kernel may reach another device: no remote copies, remote signals or barrier semaphores. Data moves between devices by JAX's collectives and lax.ppermute only.
A program may use at most 192 MiB of HBM per device.

```python
import math
import jax
import jax.numpy as jnp
import numpy as np
from jax import lax

D = 768
HEADS = 24
HEADDIM = 64
NSTATE = 128
CONVK = 4
GROUP = 256
DI = 1536
CONVD = 1792
EPROJ = 3352
SEQLEN = 1024
NSEQ = 16
N_CTX = 4


def block_levels(rng, extent, shards, low, high):
    level = 1.0
    for axis_at, shards_of in shards:
        draws = jax.random.uniform(jax.random.fold_in(jax.random.fold_in(rng, 6), axis_at), (shards_of,), jnp.float32, low / len(shards), high / len(shards))
        level = level * jnp.repeat(jnp.exp(draws), extent[axis_at] // shards_of).reshape((-1,) + (1,) * (len(extent) - 1 - axis_at))
    return level


def length_profile(number_of, total, most, skew):
    portions = [(1 << 20) // math.isqrt(grade ** skew) + 1 for grade in range(2, number_of + 1)]
    spare, counts = total - most - (number_of - 1), [1] * (number_of - 1)
    while spare > 0:
        free = [i for i in range(number_of - 1) if counts[i] < most]
        pool, remaining = sum([portions[i] for i in free]), spare
        for i in free:
            extra = min(most - counts[i], max(1, remaining * portions[i] // pool), spare)
            counts[i] = counts[i] + extra
            spare = spare - extra
    return np.array([most] + counts)


def uneven_parts(stream_key, count, total, limit, skew):
    if count == 2:
        one = jax.random.randint(stream_key, (), max(1, total - limit), min(limit, total - 1) + 1)
        return jnp.stack([one, total - one])
    lengths = jnp.asarray(length_profile(count, total, limit, skew), jnp.int32)
    twos = (count - 1) // 2
    giver, receiver = lengths[1:1 + 2 * twos:2], lengths[2:2 + 2 * twos:2]
    margin = jnp.minimum(giver - 1, limit - receiver)
    shifted = jax.random.randint(jax.random.fold_in(stream_key, 1), (twos,), 0, 1 << 20) % (margin + 1)
    lengths = lengths.at[1:1 + 2 * twos:2].set(giver - shifted).at[2:2 + 2 * twos:2].set(receiver + shifted)
    return lengths[jax.random.permutation(jax.random.fold_in(stream_key, 2), count)]


def gaussian(own_key, shape, deviation, most, cuts=(), kind=jnp.bfloat16):
    values = deviation * jax.random.normal(own_key, shape, jnp.float32)
    if cuts:
        values = values * block_levels(own_key, shape, cuts, -0.22, 0.18)
    return jnp.clip(values, -most, most).astype(kind)


def setup_inputs(seed: int = 0) -> dict:
    splits = jax.random.split(jax.random.key(seed), 15)
    tokens = gaussian(splits[0], (NSEQ, SEQLEN, D), 1.0, 6.0, ((0, 8), (1, 4)))
    segment_ids = jax.vmap(lambda own: jnp.searchsorted(jnp.cumsum(uneven_parts(own, 4, SEQLEN, SEQLEN // 2, 2)), jnp.arange(SEQLEN), side="right"))(jax.random.split(splits[1], NSEQ)).reshape((NSEQ, SEQLEN)).astype(jnp.int32)
    cotangent = gaussian(splits[2], (NSEQ, SEQLEN, D), 1.0, 6.0, ((0, 8), (1, 4)))
    w_in = gaussian(splits[3], (D, EPROJ), D ** -0.5, 0.21875, ((0, 32),), jnp.float32)
    w_out = gaussian(splits[4], (DI, D), DI ** -0.5, 0.15625, ((0, 32),), jnp.float32)
    mom_in = gaussian(splits[5], (D, EPROJ), 24.0, 128.0, ((0, 32),), jnp.float32)
    mom_out = gaussian(splits[6], (DI, D), 100.0, 640.0, ((0, 32),), jnp.float32)
    pre_gain = jnp.clip(1.0 + 0.1 * jax.random.normal(splits[7], (D,), jnp.float32), 0.5, 1.5)
    conv_weight = gaussian(splits[8], (CONVK, CONVD), CONVK ** -0.5, 3.0, (), jnp.float32)
    conv_bias = gaussian(splits[9], (CONVD,), 0.5, 6.0, (), jnp.float32)
    dt_bias = jnp.clip(jax.random.uniform(splits[10], (HEADS,), jnp.float32, -5.0, -3.0), -5.0, -3.0)
    a_log = jnp.clip(jax.random.uniform(splits[11], (HEADS,), jnp.float32, -3.5, 1.1), -3.5, 1.1)
    d_skip = jnp.clip(jax.random.uniform(splits[12], (HEADS,), jnp.float32, 0.5, 1.5), 0.5, 1.5)
    norm_gain = jnp.clip(1.0 + 0.1 * jax.random.normal(splits[13], (DI,), jnp.float32), 0.5, 1.5)
    return dict(tokens=tokens, segment_ids=segment_ids, cotangent=cotangent, w_in=w_in, w_out=w_out, mom_in=mom_in, mom_out=mom_out, pre_gain=pre_gain, conv_weight=conv_weight, conv_bias=conv_bias, dt_bias=dt_bias, a_log=a_log, d_skip=d_skip, norm_gain=norm_gain)


norm_eps = 1e-05
coef_a = 3.4445
coef_b = -4.775
coef_c = 2.0315
momentum_rate = 0.95
muon_rate = 0.05
plain_rate = 0.003

@jax.custom_vjp
def low(v):
    return lax.optimization_barrier(v.astype(jnp.bfloat16)).astype(jnp.float32)

@jax.custom_vjp
def low_back(v):
    return v

def low_keep(v):
    return (low(v), None)

def low_pass(kept, grad):
    return (grad,)

def back_keep(v):
    return (v, None)

def back_low(kept, grad):
    return (low(grad),)
low.defvjp(low_keep, low_pass)
low_back.defvjp(back_keep, back_low)

def pre_norm(x_float, gain_vec):
    mean_sq = lax.optimization_barrier(jnp.mean(x_float * x_float, axis=-1, keepdims=True))
    return x_float * lax.rsqrt(mean_sq + norm_eps) * gain_vec

def make_masks(seg_float, rim_seg):
    block_len = seg_float.shape[1]
    causal = jnp.arange(block_len)[:, None] >= jnp.arange(block_len)[None, :]
    same_seg = jnp.where(causal[None], seg_float[:, :, None] == seg_float[:, None, :], False).astype(jnp.float32)
    end_same = (seg_float == seg_float[:, -1:]).astype(jnp.float32)
    carry_mask = (seg_float == rim_seg[:, -1:]).astype(jnp.float32)
    seg_ext = jnp.concatenate([rim_seg, seg_float], axis=1)
    tap_masks = tuple(((seg_ext[:, tap_idx:tap_idx + block_len] == seg_float).astype(jnp.float32) for tap_idx in range(CONVK - 1)))
    return (same_seg, end_same, carry_mask, tap_masks)

def block_mid(seg_masks, conv_in, dt_raw, rim_vals, conv_weight, conv_bias, dt_bias, a_log):
    same_seg, end_same, carry_mask, tap_masks = seg_masks
    batch_rows = conv_in.shape[0]
    block_len = conv_in.shape[1]
    extended = jnp.concatenate([rim_vals, conv_in], axis=1)
    conv_sum = conv_bias + conv_weight[CONVK - 1] * conv_in
    for tap_idx in range(CONVK - 1):
        conv_sum = conv_sum + conv_weight[tap_idx] * extended[:, tap_idx:tap_idx + block_len, :] * tap_masks[tap_idx][..., None]
    activated = jax.nn.silu(conv_sum)
    x_heads = activated[..., :DI].reshape(batch_rows, block_len, HEADS, HEADDIM)
    b_state = activated[..., DI:DI + NSTATE]
    c_state = activated[..., DI + NSTATE:]
    dt_step = jax.nn.softplus(dt_raw + dt_bias)
    log_decay = -dt_step * jnp.exp(a_log)
    cum_decay = jnp.cumsum(log_decay, axis=1)
    block_decay = jnp.exp(cum_decay[:, -1, :]) * carry_mask[:, -1:]
    end_weights = jnp.exp(cum_decay[:, -1:, :] - cum_decay) * end_same[..., None] * dt_step
    local_state = jnp.einsum('bqh,bqhp,bqn->bhpn', end_weights, x_heads, b_state, precision=lax.Precision.HIGHEST)
    return (block_decay, local_state, x_heads, b_state, c_state, dt_step, cum_decay)

def block_out(seg_masks, x_heads, b_state, c_state, dt_step, cum_decay, incoming, gate_in, d_skip, norm_gain):
    same_seg, end_same, carry_mask, tap_masks = seg_masks
    batch_rows = x_heads.shape[0]
    block_len = x_heads.shape[1]
    scores = jnp.einsum('btn,bsn->bts', c_state, b_state, precision=lax.Precision.HIGHEST)
    cum_heads = jnp.swapaxes(cum_decay, 1, 2)
    decay_gap = cum_heads[:, :, :, None] - cum_heads[:, :, None, :]
    keep_mask = same_seg[:, None]
    decay_mat = jnp.exp(jnp.where(keep_mask > 0, decay_gap, 0.0)) * keep_mask
    weight = decay_mat * scores[:, None] * jnp.swapaxes(dt_step, 1, 2)[:, :, None, :]
    y_inner = jnp.einsum('bhts,bshp->bthp', weight, x_heads, precision=lax.Precision.HIGHEST)
    y_carry = jnp.einsum('btn,bhpn->bthp', c_state, incoming, precision=lax.Precision.HIGHEST)
    y_carry = y_carry * (jnp.exp(cum_decay) * carry_mask[..., None])[..., None]
    y_heads = y_inner + y_carry + d_skip[:, None] * x_heads
    gated = y_heads.reshape(batch_rows, block_len, DI) * jax.nn.silu(gate_in)
    return gated * lax.rsqrt(lax.optimization_barrier(jnp.mean(gated * gated, axis=-1, keepdims=True)) + norm_eps) * norm_gain

def orthogonal(matrix_low):
    frobenius = jnp.sqrt(jnp.sum(jnp.square(matrix_low.astype(jnp.float32))))
    current = (matrix_low.astype(jnp.float32) / (frobenius + 1e-07)).astype(jnp.bfloat16)
    for turn_idx in range(5):
        gram_mat = jnp.dot(current, current.T, preferred_element_type=jnp.float32).astype(jnp.bfloat16)
        poly_mat = coef_b * gram_mat.astype(jnp.float32) + coef_c * jnp.dot(gram_mat, gram_mat, preferred_element_type=jnp.float32)
        poly_mat = poly_mat.astype(jnp.bfloat16)
        current = (coef_a * current.astype(jnp.float32) + jnp.dot(poly_mat, current, preferred_element_type=jnp.float32)).astype(jnp.bfloat16)
    return current

def reference(tokens, segment_ids, cotangent, w_in, w_out, mom_in, mom_out, pre_gain, conv_weight, conv_bias, dt_bias, a_log, d_skip, norm_gain):
    seg_all = segment_ids.astype(jnp.float32)
    rim_rows = CONVK - 1

    def forward(x_float, w_in, w_out, pre_gain, conv_weight, conv_bias, dt_bias, a_log, d_skip, norm_gain):
        win_low = low(w_in)
        wout_low = low(w_out)

        def one_sequence(pair_in):
            x_seq, seg_seq = pair_in
            normed = pre_norm(x_seq, pre_gain)
            projected = jnp.dot(low(normed), win_low, precision=lax.Precision.HIGHEST, preferred_element_type=jnp.float32)
            projected = low_back(low(projected)).reshape(N_CTX, GROUP, EPROJ)
            gate_in = projected[..., :DI]
            conv_in = projected[..., DI:DI + CONVD]
            dt_raw = projected[..., DI + CONVD:]
            seg_blocks = seg_seq.reshape(N_CTX, GROUP)
            rim_vals = jnp.concatenate([jnp.zeros((1, rim_rows, CONVD), jnp.float32), conv_in[:-1, GROUP - rim_rows:, :]], axis=0)
            rim_seg = jnp.concatenate([jnp.zeros((1, rim_rows), jnp.float32), seg_blocks[:-1, GROUP - rim_rows:]], axis=0)
            seg_masks = make_masks(seg_blocks, rim_seg)
            block_decay, local_state, x_heads, b_state, c_state, dt_step, cum_decay = block_mid(seg_masks, conv_in, dt_raw, rim_vals, conv_weight, conv_bias, dt_bias, a_log)

            def advance(state_now, item_pair):
                dec_vec, loc_state = item_pair
                return (dec_vec[:, None, None] * state_now + loc_state, state_now)
            _, incoming = lax.scan(advance, jnp.zeros((HEADS, HEADDIM, NSTATE), jnp.float32), (block_decay, local_state))
            gated_normed = block_out(seg_masks, x_heads, b_state, c_state, dt_step, cum_decay, incoming, gate_in, d_skip, norm_gain)
            branch = jnp.dot(low(gated_normed.reshape(SEQLEN, DI)), wout_low, precision=lax.Precision.HIGHEST, preferred_element_type=jnp.float32)
            return x_seq + branch
        return lax.map(jax.checkpoint(one_sequence), (x_float, seg_all))
    x_float = tokens.astype(jnp.float32)
    result, backward = jax.vjp(forward, x_float, w_in, w_out, pre_gain, conv_weight, conv_bias, dt_bias, a_log, d_skip, norm_gain)
    gradients = backward(cotangent.astype(jnp.float32))
    g_tokens, grad_w_in, grad_w_out, grad_pre, grad_convw, grad_convb, grad_dtb, grad_alog, grad_skip, grad_norm = gradients
    new_mom_in = momentum_rate * mom_in + grad_w_in
    new_mom_out = momentum_rate * mom_out + grad_w_out
    ortho_in = orthogonal(new_mom_in.astype(jnp.bfloat16))
    ortho_out = orthogonal(new_mom_out.astype(jnp.bfloat16).T).T
    new_w_in = w_in - muon_rate * 0.2 * math.sqrt(max(D, EPROJ)) * ortho_in.astype(jnp.float32)
    new_w_out = w_out - muon_rate * 0.2 * math.sqrt(max(DI, D)) * ortho_out.astype(jnp.float32)
    return (result.astype(jnp.bfloat16), g_tokens.astype(jnp.bfloat16), grad_w_in, grad_w_out, grad_pre, grad_convw, grad_convb, grad_dtb, grad_alog, grad_skip, grad_norm, new_w_in, new_w_out, new_mom_in, new_mom_out, pre_gain - plain_rate * grad_pre, conv_weight - plain_rate * grad_convw, conv_bias - plain_rate * grad_convb, dt_bias - plain_rate * grad_dtb, a_log - plain_rate * grad_alog, d_skip - plain_rate * grad_skip, norm_gain - plain_rate * grad_norm)
```

```python
from functools import partial
import math

import jax
import jax.numpy as jnp
from jax import lax
from jax.experimental import pallas as pl
from jax.experimental.pallas import tpu as pltpu
from jax.sharding import Mesh, PartitionSpec as P

D = 768
HEADS = 24
HEADDIM = 64
NSTATE = 128
CONVK = 4
DI = 1536
CONVD = 1792
EPROJ = 3352
CHUNK = 256
TILE = 256
TILES = DI // TILE
HALO = 16
CPAD = 2048
RANGE = 60.0

norm_eps = 1e-05
coef_a = 3.4445
coef_b = -4.775
coef_c = 2.0315
momentum_rate = 0.95
muon_rate = 0.05
plain_rate = 0.003

INTERPRET = False
bf16 = jnp.bfloat16
f32 = jnp.float32
HIGH = lax.Precision.HIGHEST


def mm(a, b):
    return lax.dot_general(a, b, (((1,), (0,)), ((), ())), preferred_element_type=f32)


def mm_nt(a, b):
    return lax.dot_general(a, b, (((1,), (1,)), ((), ())), preferred_element_type=f32)


def mm_tn(a, b):
    return lax.dot_general(a, b, (((0,), (0,)), ((), ())), preferred_element_type=f32)


def mm_high(a, b):
    return lax.dot_general(
        a, b, (((1,), (0,)), ((), ())), precision=HIGH, preferred_element_type=f32
    )


def mm_nt_high(a, b):
    return lax.dot_general(
        a, b, (((1,), (1,)), ((), ())), precision=HIGH, preferred_element_type=f32
    )


def mm_tn_high(a, b):
    return lax.dot_general(
        a, b, (((0,), (0,)), ((), ())), precision=HIGH, preferred_element_type=f32
    )


def iota(shape, dim):
    return lax.broadcasted_iota(jnp.int32, shape, dim)


def sigmoid(v):
    return 1.0 / (1.0 + jnp.exp(-v))


def split2(v):
    hi = v.astype(bf16)
    return hi, (v - hi.astype(f32)).astype(bf16)


def conv_sum(v, aux, cw):
    acc = cw[4:5, :] + cw[3:4, :] * v[HALO:, :]
    for j in range(3):
        acc = acc + cw[j : j + 1, :] * (pltpu.roll(v, 3 - j, 0)[HALO:, :] * aux[:, j : j + 1])
    return acc


def conv_back(g, v, aux, cw):
    width = g.shape[1]
    rows = v.shape[0]
    head = jnp.zeros((HALO, width), f32)
    out = cw[3:4, :] * jnp.concatenate([head, g], axis=0)
    taps = []
    for j in range(3):
        masked = g * aux[:, j : j + 1]
        taps.append(jnp.sum(masked * pltpu.roll(v, 3 - j, 0)[HALO:, :], axis=0, keepdims=True))
        back = jnp.concatenate([head, cw[j : j + 1, :] * masked], axis=0)
        out = out + pltpu.roll(back, rows - (3 - j), 0)
    taps.append(jnp.sum(g * v[HALO:, :], axis=0, keepdims=True))
    taps.append(jnp.sum(g, axis=0, keepdims=True))
    return out, taps


def chunk_mask(aux, segrow, k):
    rows = slice(k * CHUNK, (k + 1) * CHUNK)
    same = aux[rows, 5:6] == segrow[0:1, rows]
    return same & (iota((CHUNK, CHUNK), 0) >= iota((CHUNK, CHUNK), 1))


def pack3(v):
    hi = v.astype(bf16).astype(f32)
    rest = v - hi
    mid = rest.astype(bf16).astype(f32)
    lane = iota(v.shape, 1)
    return jnp.where(lane < 32, hi, jnp.where(lane < 64, mid, rest - mid)).astype(bf16)


def spread(width, first):
    lane = iota((128, width), 0)
    head = first + iota((128, width), 1) // HEADDIM
    return jnp.where(((lane & 31) == head) & (lane < 96), 1.0, 0.0).astype(bf16)


def gather_heads(width, first):
    return jnp.where(
        iota((width, 128), 1) == first + iota((width, 128), 0) // HEADDIM, 1.0, 0.0
    )


def head_sum(v, picks):
    hi, lo = split2(v)
    return mm(hi, picks) + mm(lo, picks)


def triangle(strict):
    r, c = iota((CHUNK, CHUNK), 0), iota((CHUNK, CHUNK), 1)
    return jnp.where((r > c) if strict else (r >= c), 1.0, 0.0)


def head_steps(bcd_ref, hp):
    raw = bcd_ref[HALO:, 256:384].astype(f32)
    raw = raw + pltpu.roll(raw, 32, 1) + pltpu.roll(raw, 64, 1)
    z = raw + hp[0:1, :]
    dt = jnp.maximum(z, 0.0) + jnp.log1p(jnp.exp(-jnp.abs(z)))
    return z, dt, -dt * hp[1:2, :]


def prelude(bcd_ref, aux_ref, segrow_ref, cwbc_ref, hp_ref, sm, pka, pkb, pkw, pke, bb, cb, dts, cums, erow, flag):
    aux, segrow, hp = aux_ref[...], segrow_ref[...], hp_ref[...]
    chunks = aux.shape[0] // CHUNK
    cs = conv_sum(bcd_ref[:, 0:256].astype(f32), aux, cwbc_ref[...])
    act = cs * sigmoid(cs)
    b_act, c_act = act[:, :NSTATE], act[:, NSTATE:]
    bb[...] = b_act.astype(bf16)
    cb[...] = c_act.astype(bf16)
    z, dt, ld = head_steps(bcd_ref, hp)
    dts[...] = dt
    lower = triangle(False)
    worst = jnp.float32(0.0)
    for k in range(chunks):
        rows = slice(k * CHUNK, (k + 1) * CHUNK)
        cum = mm_high(lower, ld[rows])
        cums[rows, :] = cum
        first, last = cum[0:1], cum[CHUNK - 1 : CHUNK]
        middle = 0.5 * (first + last)
        worst = jnp.maximum(worst, jnp.max(0.5 * (first - last)))
        carry = jnp.exp(cum) * aux[rows, 3:4]
        pka[rows, :] = pack3(jnp.exp(jnp.minimum(middle - cum, RANGE)) * dt[rows])
        pkb[rows, :] = pack3(jnp.exp(jnp.minimum(cum - middle, RANGE)))
        pkw[rows, :] = pack3(jnp.exp(last - cum) * aux[rows, 4:5] * dt[rows])
        pke[rows, :] = pack3(carry)
        erow[8 * k : 8 * k + 8, :] = carry[CHUNK - 8 :, :]
        scores = mm_nt_high(c_act[rows], b_act[rows])
        sm[k] = jnp.where(chunk_mask(aux, segrow, k), scores, 0.0).astype(bf16)
    flag[0] = jnp.where(worst > RANGE, 1, 0)


def decay_matrix(cum, head):
    pick = iota((CHUNK, 128), 1) == head
    col = jnp.sum(jnp.where(pick, cum, 0.0), axis=1, keepdims=True)
    one = jnp.where(iota((8, 128), 1) == head, 1.0, 0.0)
    row = mm_nt_high(one, cum)[0:1]
    return jnp.exp(jnp.minimum(col - row, 0.0))


def state_decay(erow, k, picks):
    return jnp.sum(picks * erow[8 * k + 7 : 8 * k + 8, :], axis=1, keepdims=True)


def local_kernel(
    x_ref, bcd_ref, aux_ref, segrow_ref, cw_ref, cwbc_ref, hp_ref,
    y_ref, s_ref, cb_ref, pkd_ref, edev_ref,
    sm, pka, pkb, pkw, pke, bb, dts, cums, erow, flag,
):
    j = pl.program_id(0)
    chunks = aux_ref.shape[0] // CHUNK

    @pl.when(j == 0)
    def _():
        prelude(bcd_ref, aux_ref, segrow_ref, cwbc_ref, hp_ref, sm, pka, pkb, pkw, pke, bb, cb_ref, dts, cums, erow, flag)
        before = jnp.ones((1, 128), f32)
        for k in range(chunks):
            rows = slice(k * CHUNK, (k + 1) * CHUNK)
            own = jnp.exp(cums[rows, :]) * aux_ref[rows, 3:4] * before
            edev_ref[rows, :] = own
            pkd_ref[rows, :] = pack3(own)
            before = own[CHUNK - 1 : CHUNK]

    first = 4 * j
    cw = cw_ref[...]
    x = conv_sum(x_ref[...].astype(f32), aux_ref[...], cw)
    x = x * sigmoid(x)
    sel = spread(TILE, first)
    picks = gather_heads(TILE, first)
    wx = (mm(pkw[...], sel) * x).astype(bf16)
    state = None
    for k in range(chunks):
        rows = slice(k * CHUNK, (k + 1) * CHUNK)
        y = cw[5:6, :] * x[rows]
        if k > 0:
            y = y + mm(pke[rows, :], sel) * mm_nt(cb_ref[rows, :], state.astype(bf16))
        y_ref[rows, :] = y
        new = mm_tn(wx[rows], bb[rows, :])
        state = new if k == 0 else state_decay(erow, k, picks) * state + new
    s_ref[...] = state

    @pl.when(flag[0] == 0)
    def _():
        xs = (mm(pka[...], sel) * x).astype(bf16)
        scale = mm(pkb[...], sel)
        for k in range(chunks):
            rows = slice(k * CHUNK, (k + 1) * CHUNK)
            y_ref[rows, :] += scale[rows] * mm(sm[k], xs[rows])

    @pl.when(flag[0] != 0)
    def _():
        dtx = x * mm(pack3(dts[...]), sel)
        for k in range(chunks):
            rows = slice(k * CHUNK, (k + 1) * CHUNK)
            for i in range(TILE // HEADDIM):
                weight = decay_matrix(cums[rows, :], first + i) * sm[k].astype(f32)
                own = iota((CHUNK, TILE), 1) // HEADDIM == i
                y_ref[rows, :] += mm(weight.astype(bf16), jnp.where(own, dtx[rows], 0.0).astype(bf16))


def gate_kernel(
    yloc_ref, gate_ref, cb_ref, pkd_ref, sin_ref, wout_ref, tok_ref, cot_ref, gain_ref,
    mixed_ref, gl_ref, gy_ref, gg_ref, gain_grad_ref, gs_ref, sel,
):
    i = pl.program_id(0)

    @pl.when(i == 0)
    def _():
        sel[...] = spread(DI, 0)
        gain_grad_ref[...] = jnp.zeros_like(gain_grad_ref)
        gs_ref[...] = jnp.zeros_like(gs_ref)

    decay = mm(pkd_ref[...], sel[...])
    y = yloc_ref[...] + decay * mm_nt(cb_ref[...], sin_ref[...])
    gate = gate_ref[...].astype(f32)
    sg = sigmoid(gate)
    sl = gate * sg
    gated = y * sl
    r = lax.rsqrt(jnp.mean(gated * gated, axis=1, keepdims=True) + norm_eps)
    gain = gain_ref[...]
    unit = gated * r
    gl = (unit * gain).astype(bf16)
    gl_ref[...] = gl
    mixed_ref[...] = (tok_ref[...].astype(f32) + mm(gl, wout_ref[...])).astype(bf16)
    back = mm_nt(cot_ref[...], wout_ref[...])
    gain_grad_ref[...] += jnp.sum(back * unit, axis=0, keepdims=True)
    back = back * gain
    back = r * (back - unit * jnp.mean(back * unit, axis=1, keepdims=True))
    gy = back * sl
    gy_ref[...] = gy
    gg_ref[...] = (back * y * (sg + sl * (1.0 - sg))).astype(bf16)
    gs_ref[...] += mm_tn((decay * gy).astype(bf16), cb_ref[...])


def back_kernel(
    x_ref, bcd_ref, aux_ref, segrow_ref, cw_ref, cwbc_ref, hp_ref, gy_ref, sin_ref, gout_ref,
    gx_ref, gbcd_ref, last_ref, rim_ref, lastbc_ref, rimbc_ref, gcw_ref, gcwbc_ref, ghp_ref,
    sm, pka, pkb, pkw, pke, bb, cb, dts, cums, erow, flag, gsm, gb, gc, pq, qi, qe, dg, gxi, pi, qq,
):
    j = pl.program_id(0)
    tokens = aux_ref.shape[0]
    chunks = tokens // CHUNK

    @pl.when(j == 0)
    def _():
        prelude(bcd_ref, aux_ref, segrow_ref, cwbc_ref, hp_ref, sm, pka, pkb, pkw, pke, bb, cb, dts, cums, erow, flag)
        for ref in (gsm, gb, gc, pq, qi, qe, dg):
            ref[...] = jnp.zeros_like(ref)

    first = 4 * j
    cw, aux = cw_ref[...], aux_ref[...]
    v = x_ref[...].astype(f32)
    cs = conv_sum(v, aux, cw)
    sg = sigmoid(cs)
    x = cs * sg
    sel = spread(TILE, first)
    picks = gather_heads(TILE, first)
    picks_low = picks.astype(bf16)
    gy = gy_ref[...]

    @pl.when(flag[0] == 0)
    def _():
        scale_x = mm(pka[...], sel)
        xs = (scale_x * x).astype(bf16)
        ys = (mm(pkb[...], sel) * gy).astype(bf16)
        for k in range(chunks):
            rows = slice(k * CHUNK, (k + 1) * CHUNK)
            gsm[k] += mm_nt(ys[rows], xs[rows])
            gxs = mm_tn(sm[k], ys[rows])
            gxi[rows, :] = scale_x[rows] * gxs
            pi[rows, :] = ys[rows].astype(f32) * mm(sm[k], xs[rows])
            qq[rows, :] = xs[rows].astype(f32) * gxs

    @pl.when(flag[0] != 0)
    def _():
        scale = mm(pack3(dts[...]), sel)
        dtx = scale * x
        gxi[...] = jnp.zeros_like(gxi)
        pi[...] = jnp.zeros_like(pi)
        qq[...] = jnp.zeros_like(qq)
        for k in range(chunks):
            rows = slice(k * CHUNK, (k + 1) * CHUNK)
            for i in range(TILE // HEADDIM):
                own = iota((CHUNK, TILE), 1) // HEADDIM == i
                decay = decay_matrix(cums[rows, :], first + i)
                weight = (decay * sm[k].astype(f32)).astype(bf16)
                xh = jnp.where(own, dtx[rows], 0.0).astype(bf16)
                yh = jnp.where(own, gy[rows], 0.0).astype(bf16)
                gsm[k] += decay * mm_nt(yh, xh)
                gxs = mm_tn(weight, yh)
                gxi[rows, :] += scale[rows] * gxs
                pi[rows, :] += yh.astype(f32) * mm(weight, xh)
                qq[rows, :] += xh.astype(f32) * gxs

    wscale = mm(pkw[...], sel)
    wx = (wscale * x).astype(bf16)
    carried = (mm(pke[...], sel) * gy).astype(bf16)
    states = [sin_ref[...].astype(f32)]
    for k in range(chunks - 1):
        rows = slice(k * CHUNK, (k + 1) * CHUNK)
        states.append(state_decay(erow, k, picks) * states[k] + mm_tn(wx[rows], bb[rows, :]))
    gstate = gout_ref[...].astype(f32)
    g_x = cw[5:6, :] * gy + gxi[...]
    parts = [None] * chunks
    for k in reversed(range(chunks)):
        rows = slice(k * CHUNK, (k + 1) * CHUNK)
        low = states[k].astype(bf16)
        glow = gstate.astype(bf16)
        gc[rows, :] += mm(carried[rows], low)
        gb[rows, :] += mm(wx[rows], glow)
        pi[rows, :] += carried[rows].astype(f32) * mm_nt(cb[rows, :], low)
        back = mm_nt(bb[rows, :], glow)
        parts[k] = g_x[rows] + wscale[rows] * back
        qe[rows, :] += head_sum(wx[rows].astype(f32) * back, picks_low)
        decay = state_decay(erow, k, picks)
        per_row = jnp.sum(gstate * states[k], axis=1, keepdims=True) * decay
        dg[8 * k : 8 * k + 1, :] += jnp.sum(per_row * picks, axis=0, keepdims=True)
        if k > 0:
            gstate = decay * gstate + mm_tn(carried[rows], cb[rows, :])
    qi[...] += head_sum(qq[...], picks_low)
    pq[...] += head_sum(pi[...], picks_low)
    g_x = jnp.concatenate(parts, axis=0)
    skip = jnp.sum(gy * x, axis=0, keepdims=True)
    g_cs = g_x * (sg + x * (1.0 - sg))
    g_in, taps = conv_back(g_cs, v, aux, cw)
    gx_ref[...] = g_in[HALO:].astype(bf16)
    last_ref[...] = g_in[tokens + HALO - 8 :]
    rim_ref[...] = g_in[HALO - 8 : HALO]
    zero = jnp.zeros((1, TILE), f32)
    gcw_ref[...] = jnp.concatenate(taps + [skip, zero, zero], axis=0)

    @pl.when(j == TILES - 1)
    def _():
        hp, segrow = hp_ref[...], segrow_ref[...]
        cwbc = cwbc_ref[...]
        vb = bcd_ref[:, 0:256].astype(f32)
        csb = conv_sum(vb, aux, cwbc)
        sgb = sigmoid(csb)
        act = csb * sgb
        z, dt, ld = head_steps(bcd_ref, hp)
        lower, under = triangle(False), triangle(True)
        gbs, gcs, lds = [], [], []
        for k in range(chunks):
            rows = slice(k * CHUNK, (k + 1) * CHUNK)
            gs = jnp.where(chunk_mask(aux, segrow, k), gsm[k], 0.0)
            gcs.append(gc[rows, :] + mm_high(gs, act[rows, :NSTATE]))
            gbs.append(gb[rows, :] + mm_tn_high(gs, act[rows, NSTATE:]))
            lds.append(
                mm_tn_high(lower, pq[rows, :] - qi[rows, :])
                + mm_high(under, qe[rows, :])
                + dg[8 * k : 8 * k + 1, :]
            )
        g_act = jnp.concatenate(
            [jnp.concatenate(gbs, axis=0), jnp.concatenate(gcs, axis=0)], axis=1
        )
        g_csb = g_act * (sgb + act * (1.0 - sgb))
        g_inb, tapsb = conv_back(g_csb, vb, aux, cwbc)
        g_ld = jnp.concatenate(lds, axis=0)
        sz = sigmoid(z)
        ratio = jnp.where(z < -15.0, 1.0, sz / jnp.where(z < -15.0, 1.0, dt))
        g_raw = (qi[...] + qe[...]) * ratio - hp[1:2, :] * g_ld * sz
        g_raw = jnp.where(iota(g_raw.shape, 1) < HEADS, g_raw, 0.0)
        gbcd_ref[:, 0:256] = g_inb[HALO:].astype(bf16)
        gbcd_ref[:, 256:384] = g_raw.astype(bf16)
        gbcd_ref[:, 384:512] = jnp.zeros((tokens, 128), bf16)
        lastbc_ref[...] = g_inb[tokens + HALO - 8 :]
        rimbc_ref[...] = g_inb[HALO - 8 : HALO]
        gcwbc_ref[...] = jnp.concatenate(tapsb + [zero, zero, zero], axis=0)
        ghp_ref[...] = jnp.concatenate(
            [
                jnp.sum(g_raw, axis=0, keepdims=True),
                jnp.sum(g_ld * ld, axis=0, keepdims=True),
                jnp.zeros((6, 128), f32),
            ],
            axis=0,
        )


BLOCK = 256


def turns_kernel(g_ref, v_ref, o_ref, G, H, Gh, Gl, Ph, Pl, Hh, Hl):
    blocks = D // BLOCK

    def each(body):
        def step(i, carry):
            body(pl.ds(pl.multiple_of(i * BLOCK, BLOCK), BLOCK))
            return carry

        lax.fori_loop(0, blocks, step, 0)

    total = jnp.float32(0.0)
    for i in range(blocks):
        rows = slice(i * BLOCK, (i + 1) * BLOCK)
        diag = iota((BLOCK, D), 1) == iota((BLOCK, D), 0) + i * BLOCK
        total = total + jnp.sum(jnp.where(diag, g_ref[rows, :], 0.0))
    scale = 1.0 / (jnp.sqrt(jnp.full((1, 128), total, f32)) + 1e-07)[0:1, 0:1]
    square = scale * scale

    def load(rows):
        G[rows, :] = g_ref[rows, :] * square

    each(load)
    v = v_ref[...] * scale
    for turn in range(5):
        fine = turn >= 3

        def halves(rows):
            hi, lo = split2(G[rows, :])
            Gh[rows, :] = hi
            if fine:
                Gl[rows, :] = lo

        each(halves)

        def poly(rows):
            g2 = mm(Gh[rows, :], Gh[...])
            if fine:
                g2 = g2 + mm(Gh[rows, :], Gl[...]) + mm(Gl[rows, :], Gh[...])
                hi, lo = split2(coef_b * G[rows, :] + coef_c * g2)
                Pl[rows, :] = lo
                Ph[rows, :] = hi
            else:
                Ph[rows, :] = (coef_b * Gh[rows, :].astype(f32) + coef_c * g2).astype(bf16)

        each(poly)
        hi, lo = split2(v)
        moved = mm(hi, Ph[...]) + mm(lo, Ph[...])
        if fine:
            moved = moved + mm(hi, Pl[...])
        v = coef_a * v + moved
        if turn == 4:
            break

        def left(rows):
            h = mm(Gh[rows, :], Ph[...])
            if fine:
                h = h + mm(Gh[rows, :], Pl[...]) + mm(Gl[rows, :], Ph[...])
            h = coef_a * G[rows, :] + h
            H[rows, :] = h
            hi, lo = split2(h)
            Hh[rows, :] = hi
            if fine:
                Hl[rows, :] = lo

        each(left)

        def right(rows):
            g = mm(Ph[rows, :], Hh[...])
            if fine:
                g = g + mm(Ph[rows, :], Hl[...]) + mm(Pl[rows, :], Hh[...])
            G[rows, :] = coef_a * H[rows, :] + g

        each(right)
    o_ref[...] = v


def turns(gram, rows):
    square = (D, D)
    return pl.pallas_call(
        turns_kernel,
        out_shape=jax.ShapeDtypeStruct(rows.shape, f32),
        in_specs=[pl.BlockSpec(memory_space=pltpu.VMEM)] * 2,
        out_specs=pl.BlockSpec(memory_space=pltpu.VMEM),
        scratch_shapes=[pltpu.VMEM(square, f32)] * 2 + [pltpu.VMEM(square, bf16)] * 6,
        name="turns",
        interpret=INTERPRET,
    )(gram, rows)


def prelude_scratch(tokens):
    chunks = tokens // CHUNK
    head = pltpu.VMEM((tokens, 128), bf16)
    full = pltpu.VMEM((tokens, 128), f32)
    return chunks, head, full


def local_part(pc, aux, segrow, cw, hp):
    tokens = aux.shape[0]
    chunks, head, full = prelude_scratch(tokens)
    whole = lambda a: pl.BlockSpec(a.shape, lambda j: (0,) * a.ndim)
    return pl.pallas_call(
        local_kernel,
        grid=(TILES,),
        in_specs=[
            pl.BlockSpec((tokens + HALO, TILE), lambda j: (0, j)),
            pl.BlockSpec((tokens + HALO, 512), lambda j: (0, 3)),
            whole(aux),
            whole(segrow),
            pl.BlockSpec((8, TILE), lambda j: (0, j)),
            pl.BlockSpec((8, TILE), lambda j: (0, TILES)),
            whole(hp),
        ],
        out_specs=[
            pl.BlockSpec((tokens, TILE), lambda j: (0, j)),
            pl.BlockSpec((TILE, NSTATE), lambda j: (j, 0)),
            pl.BlockSpec((tokens, 128), lambda j: (0, 0)),
            pl.BlockSpec((tokens, 128), lambda j: (0, 0)),
            pl.BlockSpec((tokens, 128), lambda j: (0, 0)),
        ],
        out_shape=[
            jax.ShapeDtypeStruct((tokens, DI), f32),
            jax.ShapeDtypeStruct((DI, NSTATE), f32),
            jax.ShapeDtypeStruct((tokens, 128), bf16),
            jax.ShapeDtypeStruct((tokens, 128), bf16),
            jax.ShapeDtypeStruct((tokens, 128), f32),
        ],
        scratch_shapes=[
            pltpu.VMEM((chunks, CHUNK, CHUNK), bf16),
            head, head, head, head, head, full, full,
            pltpu.VMEM((8 * chunks, 128), f32),
            pltpu.SMEM((1,), jnp.int32),
        ],
        name="local",
        interpret=INTERPRET,
    )(pc, pc, aux, segrow, cw, cw, hp)


def gate_part(yloc, gate, cb, pkd, sin, wout, tok, cot, gain):
    tokens = yloc.shape[0]
    rows = 128
    by_row = lambda width: pl.BlockSpec((rows, width), lambda i: (i, 0))
    fixed = lambda shape: pl.BlockSpec(shape, lambda i: (0, 0))
    return pl.pallas_call(
        gate_kernel,
        grid=(tokens // rows,),
        in_specs=[
            by_row(DI), by_row(DI), by_row(128), by_row(128), fixed((DI, NSTATE)),
            fixed((DI, D)), by_row(D), by_row(D), fixed((1, DI)),
        ],
        out_specs=[
            by_row(D), by_row(DI), by_row(DI), by_row(DI), fixed((1, DI)), fixed((DI, NSTATE)),
        ],
        out_shape=[
            jax.ShapeDtypeStruct((tokens, D), bf16),
            jax.ShapeDtypeStruct((tokens, DI), bf16),
            jax.ShapeDtypeStruct((tokens, DI), f32),
            jax.ShapeDtypeStruct((tokens, DI), bf16),
            jax.ShapeDtypeStruct((1, DI), f32),
            jax.ShapeDtypeStruct((DI, NSTATE), f32),
        ],
        scratch_shapes=[pltpu.VMEM((128, DI), bf16)],
        name="gate",
        interpret=INTERPRET,
    )(yloc, gate, cb, pkd, sin, wout, tok, cot, gain)


def back_part(pc, aux, segrow, cw, hp, gy, sin, gout):
    tokens = aux.shape[0]
    chunks, head, full = prelude_scratch(tokens)
    tile = pltpu.VMEM((tokens, TILE), f32)
    whole = lambda a: pl.BlockSpec(a.shape, lambda j: (0,) * a.ndim)
    col = lambda r: pl.BlockSpec((r, TILE), lambda j: (0, j))
    fixed = lambda r, w: pl.BlockSpec((r, w), lambda j: (0, 0))
    return pl.pallas_call(
        back_kernel,
        grid=(TILES,),
        in_specs=[
            col(tokens + HALO),
            pl.BlockSpec((tokens + HALO, 512), lambda j: (0, 3)),
            whole(aux),
            whole(segrow),
            col(8),
            pl.BlockSpec((8, TILE), lambda j: (0, TILES)),
            whole(hp),
            col(tokens),
            pl.BlockSpec((TILE, NSTATE), lambda j: (j, 0)),
            pl.BlockSpec((TILE, NSTATE), lambda j: (j, 0)),
        ],
        out_specs=[
            col(tokens), fixed(tokens, 512), col(8), col(8), fixed(8, TILE), fixed(8, TILE),
            col(8), fixed(8, TILE), fixed(8, 128),
        ],
        out_shape=[
            jax.ShapeDtypeStruct((tokens, DI), bf16),
            jax.ShapeDtypeStruct((tokens, 512), bf16),
            jax.ShapeDtypeStruct((8, DI), f32),
            jax.ShapeDtypeStruct((8, DI), f32),
            jax.ShapeDtypeStruct((8, TILE), f32),
            jax.ShapeDtypeStruct((8, TILE), f32),
            jax.ShapeDtypeStruct((8, DI), f32),
            jax.ShapeDtypeStruct((8, TILE), f32),
            jax.ShapeDtypeStruct((8, 128), f32),
        ],
        scratch_shapes=[
            pltpu.VMEM((chunks, CHUNK, CHUNK), bf16),
            head, head, head, head, head, head, full, full,
            pltpu.VMEM((8 * chunks, 128), f32),
            pltpu.SMEM((1,), jnp.int32),
            pltpu.VMEM((chunks, CHUNK, CHUNK), f32),
            full, full, full, full, full,
            pltpu.VMEM((8 * chunks, 128), f32),
            tile, tile, tile,
        ],
        name="back",
        interpret=INTERPRET,
    )(pc, pc, aux, segrow, cw, cw, hp, gy, sin, gout)


CTX = ("y", "c")


def size(axis):
    return lax.axis_size(axis)


def shifted(block, axis, by):
    n = size(axis)
    return lax.ppermute(block, axis, [(i, (i + by) % n) for i in range(n)])


def swap(block):
    return lax.ppermute(block, "c", [(0, 1), (1, 0)])


def pick(block, index, axis=0):
    return lax.dynamic_index_in_dim(block, index, axis, keepdims=False)


def in_core_order(mine, other, core, axis):
    joined = jnp.concatenate([mine, other], axis=axis)
    turned = jnp.concatenate([other, mine], axis=axis)
    return jnp.where(core == 0, joined, turned)


def collect(block, axis):
    return jnp.stack([block] + [shifted(block, axis, k) for k in range(1, size(axis))])


def gather_chips(pair):
    both = collect(pair, "z")
    first, second = both[:, 0], both[:, 1]
    first, second = collect(first, "x"), collect(second, "y")
    return collect(first, "y"), collect(second, "x")


def absolute(block, names):
    for at, axis in enumerate(names):
        order = (lax.axis_index(axis) - jnp.arange(size(axis))) % size(axis)
        block = jnp.take(block, order, axis=at)
    return block


def chip_rows(block, names):
    block = absolute(block, names)
    order = [names.index(a) for a in ("z", "x", "y")]
    block = jnp.transpose(block, order + list(range(3, block.ndim)))
    return block


def fold(block, axis, at):
    me, n = lax.axis_index(axis), size(axis)
    total = pick(block, me, at)
    for k in range(1, n):
        part = pick(block, (me + k) % n, at).astype(bf16)
        total = total + shifted(part, axis, k).astype(f32)
    return total


def scatter_chips(first, second):
    first, second = fold(first, "x", 1), fold(second, "y", 2)
    first, second = fold(first, "y", 1), fold(second, "x", 1)
    return fold(jnp.stack([first, second]), "z", 1)


def total_over(block, axis):
    n = size(axis)
    if n & (n - 1):
        return jnp.sum(absolute(collect(block, axis), (axis,)), axis=0)
    step = 1
    while step < n:
        block = block + lax.ppermute(block, axis, [(i, i ^ step) for i in range(n)])
        step *= 2
    return block


def routes(seqs):
    ranks = size("y") * size("c")
    runs = ranks // seqs
    return [
        [(i, ((i % seqs + r) % seqs) * runs + i // seqs) for i in range(ranks)]
        for r in range(seqs)
    ]


def to_runs(block):
    seqs = block.shape[0]
    runs = size("y") * size("c") // seqs
    me = lax.axis_index(CTX)
    got = [
        lax.ppermute(pick(block, (me + r) % seqs), CTX, route)
        for r, route in enumerate(routes(seqs))
    ]
    order = (me // runs - jnp.arange(seqs)) % seqs
    got = jnp.take(jnp.stack(got), order, axis=0)
    return got.reshape((-1,) + block.shape[2:])


def from_runs(block, seqs):
    runs = size("y") * size("c") // seqs
    me = lax.axis_index(CTX)
    block = block.reshape((seqs, -1) + block.shape[1:])
    got = [
        lax.ppermute(pick(block, (me // runs - r) % seqs), CTX, [(b, a) for a, b in route])
        for r, route in enumerate(routes(seqs))
    ]
    order = (jnp.arange(seqs) - me) % seqs
    return jnp.take(jnp.stack(got), order, axis=0)


def along_run(block, seqs, by):
    ranks = size("y") * size("c")
    runs = ranks // seqs
    route = [(i, i + by) for i in range(ranks) if 0 <= i + by < ranks and (i + by) // runs == i // runs]
    return lax.ppermute(block, CTX, route)


def widen_in(w):
    tail = jnp.pad(w[:, DI:], ((0, 0), (0, CPAD - (EPROJ - DI))))
    return w[:, :DI], tail


def halves(block, core, axis):
    width = block.shape[axis] // 2
    mine = lax.dynamic_slice_in_dim(block, core * width, width, axis)
    other = lax.dynamic_slice_in_dim(block, (1 - core) * width, width, axis)
    return mine, other


def pair_rows(block, core, axis):
    mine, other = halves(block, core, axis)
    return in_core_order(mine[None], swap(other)[None], core, 0)


def two_colours(block):
    half = block.shape[-1] // 2
    return jnp.stack([block[..., :half], block[..., half:]])


def body(
    tokens, segment_ids, cotangent, w_in, w_out, mom_in, mom_out,
    pre_gain, conv_weight, conv_bias, dt_bias, a_log, d_skip, norm_gain,
):
    seqs = tokens.shape[0]
    core = lax.axis_index("c")
    runs = size("y") * size("c") // seqs
    place = lax.axis_index(CTX) % runs
    rows_in, rows_out = w_in.shape[0], w_out.shape[0]
    half_out = rows_out // 2

    gate_low, tail_low = widen_in(w_in.astype(bf16))
    tail_pair = pair_rows(tail_low, core, 1)
    conv_a, conv_b = gather_chips(two_colours(tail_pair))
    gate_pair = pair_rows(gate_low, core, 1)
    out_pair = pair_rows(w_out.astype(bf16), core, 0)
    gate_a, out_b = gather_chips(jnp.stack([gate_pair, out_pair]))

    def columns(a):
        return a.reshape(D, a.shape[-1])

    conv_half = jnp.concatenate(
        [columns(chip_rows(conv_a, ("y", "x", "z"))), columns(chip_rows(conv_b, ("x", "y", "z")))],
        axis=1,
    )
    w_conv = in_core_order(conv_half, swap(conv_half), core, 1)
    gate_half = columns(chip_rows(gate_a, ("y", "x", "z")))
    w_gate = in_core_order(gate_half, swap(gate_half), core, 1)
    out_half = chip_rows(out_b, ("x", "y", "z"))
    out_half = out_half.reshape(-1, 1, half_out, D)
    w_outs = in_core_order(out_half, swap(out_half), core, 1).reshape(DI, D)

    tok = to_runs(tokens)
    seg = to_runs(segment_ids.astype(f32)[..., None])
    cot = to_runs(cotangent)
    count = tok.shape[0]
    rim_tok = along_run(tok[count - HALO :], seqs, 1)
    rim_seg = along_run(seg[count - 8 :], seqs, 1)[8 - (CONVK - 1) :]
    tok_ext = jnp.concatenate([rim_tok, tok], axis=0)

    x_ext = tok_ext.astype(f32)
    inv_rms = lax.rsqrt(jnp.mean(x_ext * x_ext, axis=1, keepdims=True) + norm_eps)
    normed = (x_ext * inv_rms * pre_gain).astype(bf16)
    own_normed = normed[HALO:]

    ext = jnp.concatenate([rim_seg, seg], axis=0)
    taps = [(ext[j : j + count] == seg).astype(f32) for j in range(CONVK - 1)]
    chunked = seg.reshape(-1, CHUNK, 1)
    before = jnp.concatenate([rim_seg[CONVK - 2 :][None], chunked[:-1, CHUNK - 1 :]], axis=0)
    carry = (chunked == before).astype(f32).reshape(count, 1)
    ends = (chunked == chunked[:, CHUNK - 1 :]).astype(f32).reshape(count, 1)
    aux = jnp.pad(jnp.concatenate(taps + [carry, ends, seg], axis=1), ((0, 0), (0, 122)))
    segrow = jnp.broadcast_to(seg.reshape(1, count), (8, count))
    skip_cols = jnp.pad(jnp.repeat(d_skip, HEADDIM), (0, CONVD - DI))
    cw = jnp.concatenate(
        [conv_weight, conv_bias[None], skip_cols[None], jnp.zeros((2, CONVD), f32)], axis=0
    )

    def lanes(v):
        return jnp.pad(jnp.tile(jnp.pad(v, (0, 8)), 3), (0, 32))

    hp = jnp.pad(jnp.stack([lanes(dt_bias), lanes(jnp.exp(a_log))]), ((0, 6), (0, 0)))

    pc = mm(normed, w_conv).astype(bf16)
    yloc, sloc, cb, pkd, edev = local_part(pc, aux, segrow, cw, hp)
    whole_decay = jnp.repeat(edev[count - 1, :HEADS], HEADDIM)[:, None]
    sin = jnp.zeros((DI, NSTATE), bf16)
    for step in range(runs - 1):
        out = sloc if step == 0 else whole_decay * sin.astype(f32) + sloc
        got = along_run(out.astype(bf16), seqs, 1)
        sin = got if runs == 2 else jnp.where(place == step + 1, got, sin)
    gate = mm(own_normed, w_gate).astype(bf16)
    mixed, gl, gy, g_gate, g_norm, gs = gate_part(
        yloc, gate, cb, pkd, sin, w_outs, tok, cot, norm_gain[None]
    )
    mixed = from_runs(mixed, seqs)

    gout = jnp.zeros((DI, NSTATE), bf16)
    for step in range(runs - 1):
        out = gs if step == 0 else whole_decay * gout.astype(f32) + gs
        got = along_run(out.astype(bf16), seqs, -1)
        gout = got if runs == 2 else jnp.where(place == runs - 2 - step, got, gout)

    gx, gbcd, last, rim, lastbc, rimbc, gcw, gcwbc, ghp = back_part(
        pc, aux, segrow, cw, hp, gy, sin, gout
    )
    borrowed = along_run(jnp.concatenate([rim, rimbc], axis=1), seqs, -1)
    fixed_last = (jnp.concatenate([last, lastbc], axis=1) + borrowed).astype(bf16)
    g_tail = jnp.concatenate([gx, gbcd], axis=1)
    g_tail = lax.dynamic_update_slice(g_tail, fixed_last, (count - 8, 0))

    nz, nx, ny = size("z"), size("x"), size("y")

    def core_sum(kept, sent):
        return kept + swap(sent.astype(bf16)).astype(f32)

    grid = (nz, nx, ny, 2 * rows_in)
    gate_keep, gate_send = halves(g_gate, core, 1)
    gate_sum = core_sum(mm_tn(own_normed, gate_keep), mm_tn(own_normed, gate_send))
    g_out = mm_tn(gl, cot).reshape(-1, 2, half_out, D)
    out_sum = core_sum(pick(g_out, core, 1), pick(g_out, 1 - core, 1))
    early = scatter_chips(gate_sum.reshape(grid + (-1,)), out_sum.reshape(grid + (-1,)))
    tail_keep, tail_send = halves(g_tail, core, 1)
    tail_sum = core_sum(mm_tn(own_normed, tail_keep), mm_tn(own_normed, tail_send))
    quarter = CPAD // 4
    late = scatter_chips(
        tail_sum[:, :quarter].reshape(grid + (-1,)), tail_sum[:, quarter:].reshape(grid + (-1,))
    )
    early = early.reshape(2, 2, rows_in, -1)
    late = late.reshape(2, 2, rows_in, -1)

    mom_gate, mom_tail = widen_in(mom_in)
    mom_early = jnp.stack([pair_rows(mom_gate, core, 1), pair_rows(mom_out, core, 0)])
    mom_late = two_colours(pair_rows(mom_tail, core, 1))
    new_early = (momentum_rate * mom_early + early).astype(bf16)
    new_late = (momentum_rate * mom_late + late).astype(bf16)
    mom_gate_a, mom_out_b = gather_chips(new_early)
    mom_conv_a, mom_conv_b = gather_chips(new_late)

    def own_rows(pair):
        return pick(pair, core, 1), swap(pick(pair, 1 - core, 1))

    early_mine, early_other = own_rows(early)
    late_mine, late_other = own_rows(late)
    sum_gate = in_core_order(early_mine[0], early_other[0], core, 1)
    sum_out = in_core_order(early_mine[1], early_other[1], core, 0)
    sum_tail = in_core_order(
        jnp.concatenate([late_mine[0], late_mine[1]], axis=1),
        jnp.concatenate([late_other[0], late_other[1]], axis=1),
        core,
        1,
    )
    sum_in = jnp.concatenate([sum_gate, sum_tail[:, : EPROJ - DI]], axis=1)
    next_mom_in = momentum_rate * mom_in + sum_in
    next_mom_out = momentum_rate * mom_out + sum_out

    m_out = mom_out_b.reshape(-1, D)
    gram_out = mm_tn(m_out, m_out)
    gram_out = gram_out + swap(gram_out)
    ortho_out = turns(gram_out, next_mom_out.astype(bf16).astype(f32))
    x_gate = mom_gate_a.reshape(D, -1)
    x_a = mom_conv_a.reshape(D, -1)
    x_b = jnp.swapaxes(mom_conv_b, 0, 1).reshape(D, -1)
    gram_in = mm_nt(x_gate, x_gate) + mm_nt(x_a, x_a) + mm_nt(x_b, x_b)
    gram_in = gram_in + swap(gram_in)
    both = 2 * rows_in
    q_rows = turns(gram_in, jnp.eye(both, D, dtype=f32))
    q_hi, q_lo = split2(q_rows)

    def apply_q(x):
        return mm(q_hi, x) + mm(q_lo, x)

    ortho_pair = jnp.concatenate([apply_q(x_gate), apply_q(x_a), apply_q(x_b)], axis=1)
    ortho_pair = ortho_pair.astype(bf16).reshape(2, rows_in, -1)
    mine = pick(ortho_pair, core)
    other = swap(pick(ortho_pair, 1 - core))
    gate_cols = DI // 2
    ortho_in = jnp.concatenate(
        [
            in_core_order(mine[:, :gate_cols], other[:, :gate_cols], core, 1),
            in_core_order(mine[:, gate_cols:], other[:, gate_cols:], core, 1)[:, : EPROJ - DI],
        ],
        axis=1,
    )
    new_w_in = w_in - muon_rate * 0.2 * math.sqrt(max(D, EPROJ)) * ortho_in.astype(f32)
    new_w_out = w_out - muon_rate * 0.2 * math.sqrt(max(DI, D)) * ortho_out.astype(bf16).astype(f32)

    g_normed = mm_nt(g_gate, w_gate) + mm_nt(g_tail, w_conv)
    x_float, rms = x_ext[HALO:], inv_rms[HALO:]
    unit = x_float * rms
    scaled = g_normed * pre_gain
    g_x = rms * (scaled - unit * jnp.mean(scaled * unit, axis=1, keepdims=True))
    d_tokens = from_runs((cot.astype(f32) + g_x).astype(bf16), seqs)

    g_pre = jnp.sum(g_normed * unit, axis=0)
    g_conv = jnp.concatenate([gcw[:5], gcwbc[:5]], axis=1)
    g_skip = jnp.sum(gcw[5].reshape(HEADS, HEADDIM), axis=1)
    parts = [g_pre, g_conv.reshape(-1), ghp[0, :HEADS], ghp[1, :HEADS], g_skip, g_norm[0]]
    flat = jnp.concatenate(parts)
    used = flat.shape[0]
    flat = jnp.pad(flat, (0, -used % 1024)).reshape(-1, 128)
    for axis in ("c", "x", "y", "z"):
        flat = total_over(flat, axis)
    flat = flat.reshape(-1)
    cuts, at = [], 0
    for part in parts:
        cuts.append(flat[at : at + part.shape[0]])
        at += part.shape[0]
    grad_pre, conv_flat, grad_dtb, grad_alog, grad_skip, grad_norm = cuts
    conv_flat = conv_flat.reshape(CONVK + 1, CONVD)
    grad_convw, grad_convb = conv_flat[:CONVK], conv_flat[CONVK]
    return (
        mixed, d_tokens, sum_in, sum_out,
        grad_pre, grad_convw, grad_convb, grad_dtb, grad_alog, grad_skip, grad_norm,
        new_w_in, new_w_out, next_mom_in, next_mom_out,
        pre_gain - plain_rate * grad_pre,
        conv_weight - plain_rate * grad_convw,
        conv_bias - plain_rate * grad_convb,
        dt_bias - plain_rate * grad_dtb,
        a_log - plain_rate * grad_alog,
        d_skip - plain_rate * grad_skip,
        norm_gain - plain_rate * grad_norm,
    )


def chip_mesh(mesh):
    dp, ctx = mesh.shape["dp"], mesh.shape["ctx"]
    deep = math.gcd(dp, 4)
    return Mesh(mesh.devices.reshape(deep, dp // deep, ctx // 2, 2), ("z", "x", "y", "c"))


def solution(mesh):
    dp, ctx, every = ("z", "x"), ("y", "c"), ("z", "x", "y", "c")
    rows = P(every, None)
    return jax.shard_map(
        body,
        mesh=chip_mesh(mesh),
        in_specs=(P(dp, ctx, None), P(dp, ctx), P(dp, ctx, None), rows, rows, rows, rows)
        + (P(),) * 7,
        out_specs=(P(dp, ctx, None), P(dp, ctx, None), rows, rows)
        + (P(),) * 7
        + (rows,) * 4
        + (P(),) * 7,
        check_vma=False,
    )
```
